32 devices in a mesh: dp: 4 (over z), tx: 2 (over y), ty: 4 (over x, core).
Axes of the slice: x: 2, y: 2, z: 4, core: 2. Of those that a mesh axis runs over, the one named last changes fastest.
Arguments:
- inputs: bfloat16 [8, 1024, 2048], P('dp', 'ty'), may hold values from -6 to 6
- lengths: int32 [8], replicated, may hold values from 1 to 1024, 5120 in all
- prompt_deal: int32 [8], replicated, may hold values from 0 to 7, each once
- block_owner: int32 [4], replicated, may hold values from 0 to 3, each once
- attn_gain: float32 [2048], replicated, may hold values from 0.5 to 1.5
- latent_gain: float32 [512], replicated, may hold values from 0.5 to 1.5
- final_gain: float32 [2048], replicated, may hold values from 0.5 to 1.5
- w_query: float32 [2048, 3072], P('dp', ('tx', 'ty')), may hold values from -4 to 4
- w_down_kv: float32 [2048, 576], P('dp'), may hold values from -0.125 to 0.125
- w_up_kv: float32 [512, 4096], P('dp', ('tx', 'ty')), may hold values from -4 to 4
- w_out: float32 [2048, 2048], P('dp', 'tx'), may hold values from -0.125 to 0.125
- w_vocab: float32 [2048, 57344], P('dp', ('tx', 'ty')), may hold values from -0.125 to 0.125
Outputs:
- hidden_out: bfloat16 [8, 1024, 2048], P('dp', 'ty', 'tx')
- logits: float32 [8, 57344], P('dp', ('tx', 'ty'))
The draws below stay inside these ranges and needn't reach their ends.
Inputs may be any that keep to these rules, and one draw needn't show every extreme that they name: `prompt_deal`: a permutation of the 8 prompts. `block_owner`: a permutation of the 4 row blocks. `lengths`: some prompt has exactly 1024 live tokens.
All inputs are finite; a program needn't handle non-finite values.
Results may differ from the reference program's by a relative error of at most 0.0065.
The reference program's roundings to bfloat16 on the way count: a program that leaves them out, or rounds other values in their place, can miss the bound.
Values may be sent and summed in bfloat16 or wider, within the bound.
A program may use at most 192 MiB of HBM per device.

```python
import math
import jax
import jax.numpy as jnp
import numpy as np
from jax import lax

D = 2048
HEADS = 16
NOPE = 128
ROPE = 64
LATENT = 512
VOCAB = 57344
LEN = 1024
GROUPS = 4
PROMPTS = 8


def draw_w_query(key, part):
    base = jax.random.normal(jax.random.fold_in(key, 1), (D, HEADS * (NOPE + ROPE)), jnp.float32)
    base = jnp.clip(base, -6.0, 6.0) * D ** (-0.5)
    return jnp.clip(base, -4.0, 4.0)


def draw_w_up_kv(key, part):
    base = jax.random.normal(jax.random.fold_in(key, 3), (LATENT, 2 * HEADS * NOPE), jnp.float32)
    base = jnp.clip(base, -6.0, 6.0) * LATENT ** (-0.5)
    return jnp.clip(base, -4.0, 4.0)


def shard_levels(stream_key, extent, pieces, low, top_value):
    def one(dim, shards_of):
        draws = jax.random.uniform(jax.random.fold_in(jax.random.fold_in(stream_key, 6), dim), (shards_of,), jnp.float32, low / len(pieces), top_value / len(pieces))
        return jnp.repeat(jnp.exp(draws), extent[dim] // shards_of).reshape((-1,) + (1,) * (len(extent) - dim - 1))

    loudness = one(*pieces[0])
    for cut in pieces[1:]:
        loudness = loudness * one(*cut)
    return loudness


def split_up(number_of, total, bound, lean):
    weights = [(1 << 20) // math.isqrt(grade ** lean) + 1 for grade in range(2, number_of + 1)]
    rest, given = total - bound - (number_of - 1), [1] * (number_of - 1)
    while rest > 0:
        candidates = [i for i in range(number_of - 1) if given[i] < bound]
        mass, remaining = sum([weights[i] for i in candidates]), rest
        for i in candidates:
            extra = min(bound - given[i], max(1, remaining * weights[i] // mass), rest)
            given[i] = given[i] + extra
            rest = rest - extra
    return np.array([bound] + given)


def ragged_sizes(stream_key, number_of, total, limit, lean):
    if number_of == 2:
        one = jax.random.randint(stream_key, (), max(1, total - limit), min(limit, total - 1) + 1)
        return jnp.stack([one, total - one])
    sizes = jnp.asarray(split_up(number_of, total, limit, lean), jnp.int32)
    couples = (number_of - 1) // 2
    giver, receiver = sizes[1:1 + 2 * couples:2], sizes[2:2 + 2 * couples:2]
    room = jnp.minimum(giver - 1, limit - receiver)
    moved = jax.random.randint(jax.random.fold_in(stream_key, 1), (couples,), 0, 1 << 20) % (room + 1)
    sizes = sizes.at[1:1 + 2 * couples:2].set(giver - moved).at[2:2 + 2 * couples:2].set(receiver + moved)
    return sizes[jax.random.permutation(jax.random.fold_in(stream_key, 2), number_of)]


def scatter_about(own_key, extent, scale, limit, pieces=(), kind=jnp.bfloat16):
    array = scale * jax.random.normal(own_key, extent, jnp.float32)
    if pieces:
        array = array * shard_levels(own_key, extent, pieces, -0.22, 0.18)
    return jnp.clip(array, -limit, limit).astype(kind)


def setup_inputs(seed: int = 0) -> dict:
    key_of = jax.random.split(jax.random.key(seed), 13)
    inputs = scatter_about(key_of[0], (PROMPTS, LEN, D), 1.0, 6.0, ((0, 4), (1, 4)))
    lengths = ragged_sizes(key_of[1], PROMPTS, PROMPTS * LEN * 5 // 8, LEN, 2).astype(jnp.int32)
    prompt_deal = jax.random.permutation(key_of[2], PROMPTS).astype(jnp.int32)
    block_owner = jax.random.permutation(key_of[3], GROUPS).astype(jnp.int32)
    attn_gain = jnp.clip(1.0 + 0.1 * jax.random.normal(key_of[4], (D,), jnp.float32), 0.5, 1.5)
    latent_gain = jnp.clip(1.0 + 0.1 * jax.random.normal(key_of[5], (LATENT,), jnp.float32), 0.5, 1.5)
    final_gain = jnp.clip(1.0 + 0.1 * jax.random.normal(key_of[6], (D,), jnp.float32), 0.5, 1.5)
    w_query = draw_w_query(jax.random.fold_in(key_of[12], 71), 0)
    w_down_kv = scatter_about(key_of[8], (D, LATENT + ROPE), D ** -0.5, 0.125, ((0, 4),), jnp.float32)
    w_up_kv = draw_w_up_kv(jax.random.fold_in(key_of[12], 71), 0)
    w_out = scatter_about(key_of[10], (D, HEADS * NOPE), (HEADS * NOPE) ** -0.5, 0.125, ((0, 4), (1, 2)), jnp.float32)
    w_vocab = scatter_about(key_of[11], (D, VOCAB), D ** -0.5, 0.125, ((0, 4), (1, 8)), jnp.float32)
    return {"inputs": inputs, "lengths": lengths, "prompt_deal": prompt_deal, "block_owner": block_owner, "attn_gain": attn_gain, "latent_gain": latent_gain, "final_gain": final_gain, "w_query": w_query, "w_down_kv": w_down_kv, "w_up_kv": w_up_kv, "w_out": w_out, "w_vocab": w_vocab}


EPS = 1e-06

def normalize(values, gain):
    wide = values.astype(jnp.float32)
    return wide * lax.rsqrt(lax.optimization_barrier(jnp.mean(wide * wide, axis=-1, keepdims=True)) + EPS) * gain

def rotate(values, position):
    half_dim = values.shape[-1] // 2
    frequency = 10000.0 ** (-jnp.arange(half_dim, dtype=jnp.float32) / half_dim)
    angles = position.astype(jnp.float32)[..., None] * frequency
    cosine = jnp.cos(angles)
    sine = jnp.sin(angles)
    first_half = values[..., :half_dim]
    second_half = values[..., half_dim:]
    return jnp.concatenate([first_half * cosine - second_half * sine, first_half * sine + second_half * cosine], axis=-1)

def reference(inputs, lengths, prompt_deal, block_owner, attn_gain, latent_gain, final_gain, w_query, w_down_kv, w_up_kv, w_out, w_vocab):
    inverse = jnp.zeros((GROUPS,), jnp.int32).at[block_owner].set(jnp.arange(GROUPS, dtype=jnp.int32))

    def logical(stored):
        block_rows = stored.shape[0] // GROUPS
        blocks = stored.reshape((GROUPS, block_rows) + stored.shape[1:])
        return jnp.take(blocks, inverse, axis=0).reshape(stored.shape).astype(jnp.bfloat16)
    query_w = logical(w_query)
    down_w = logical(w_down_kv)
    up_w = logical(w_up_kv)
    out_w = logical(w_out)
    vocab_w = logical(w_vocab)
    live_len = jnp.take(lengths, prompt_deal).astype(jnp.int32)
    position = jnp.arange(LEN, dtype=jnp.int32)
    score_scale = (NOPE + ROPE) ** (-0.5)

    def one_prompt(packed):
        tokens, live = packed
        normed = normalize(tokens, attn_gain).astype(jnp.bfloat16)
        queries = jnp.dot(normed, query_w, preferred_element_type=jnp.float32).reshape(LEN, HEADS, NOPE + ROPE)
        queries = jnp.concatenate([queries[..., :NOPE], rotate(queries[..., NOPE:], position[:, None])], axis=-1).astype(jnp.bfloat16)
        down_proj = jnp.dot(normed, down_w, preferred_element_type=jnp.float32)
        latent = normalize(down_proj[:, :LATENT], latent_gain).astype(jnp.bfloat16)
        key_rope = rotate(down_proj[:, LATENT:], position).astype(jnp.bfloat16)
        key_val = jnp.dot(latent, up_w, preferred_element_type=jnp.float32).astype(jnp.bfloat16).reshape(LEN, HEADS, 2, NOPE)
        key_nope = key_val[:, :, 0].astype(jnp.float32)
        values = key_val[:, :, 1].astype(jnp.float32)
        query_wide = queries.astype(jnp.float32)
        scores = (jnp.einsum('qhd,khd->hqk', query_wide[..., :NOPE], key_nope) + jnp.einsum('qhd,kd->hqk', query_wide[..., NOPE:], key_rope.astype(jnp.float32))) * score_scale
        allowed = (position[None, :] <= position[:, None]) & (position[None, :] < live)
        scores = jnp.where(allowed[None], scores, -1e+30)
        top = lax.optimization_barrier(jnp.max(scores, axis=-1, keepdims=True))
        expo = jnp.exp(scores - top)
        softmax_w = (expo / lax.optimization_barrier(jnp.sum(expo, axis=-1, keepdims=True))).astype(jnp.bfloat16)
        attended = jnp.einsum('hqk,khd->qhd', softmax_w.astype(jnp.float32), values).astype(jnp.bfloat16).reshape(LEN, HEADS * NOPE)
        branch = lax.dot_general(attended, out_w, (((1,), (1,)), ((), ())), preferred_element_type=jnp.float32)
        layer_out = (tokens.astype(jnp.float32) + branch).astype(jnp.bfloat16)
        last_row = lax.dynamic_slice_in_dim(layer_out, live - 1, 1, 0)[0]
        return (layer_out, last_row)
    hidden_out, last_rows = lax.map(one_prompt, (inputs, live_len))
    final_rows = normalize(last_rows, final_gain).astype(jnp.bfloat16)
    logits = jnp.dot(final_rows, vocab_w, preferred_element_type=jnp.float32)
    return (hidden_out, logits)
```

```python
import functools

import jax
import jax.numpy as jnp
from jax import lax
from jax.experimental import pallas as pl
from jax.experimental.pallas import tpu as pltpu
from jax.sharding import PartitionSpec as P

NOPE = 128
ROPE = 64
LATENT = 512
LEN = 1024
TILE = 256
EPS = 1e-06


def normalize(values, gain):
    wide = values.astype(jnp.float32)
    return wide * lax.rsqrt(jnp.mean(wide * wide, axis=-1, keepdims=True) + EPS) * gain


def dot32(left, right):
    return jnp.dot(left, right, preferred_element_type=jnp.float32)


def layer_kernel(
    groups, heads, inv_ref, live_ref, x_ref, again_ref, lgain_ref, cos_ref, sin_ref,
    wq_ref, wa_ref, wb_ref, o_ref, h_ref, up_ref, k_ref, v_ref,
):
    prompt, tile = pl.program_id(0), pl.program_id(1)
    width = x_ref.shape[-1]
    rows = width // groups
    up_rows = LATENT // groups

    @pl.when((prompt == 0) & (tile == 0))
    def _():
        for g in range(groups):
            start = pl.multiple_of(inv_ref[g] * up_rows, up_rows)
            up_ref[g * up_rows : (g + 1) * up_rows, :] = wb_ref[pl.ds(start, up_rows), :]

    h_ref[...] = normalize(x_ref[0], again_ref[...]).astype(jnp.bfloat16)

    def project(w_ref):
        total = None
        for g in range(groups):
            start = pl.multiple_of(inv_ref[g] * rows, rows)
            part = dot32(h_ref[:, g * rows : (g + 1) * rows], w_ref[pl.ds(start, rows), :])
            total = part if total is None else total + part
        return total

    cosine, sine = cos_ref[...], sin_ref[...]
    lane = lax.broadcasted_iota(jnp.int32, (TILE, 128), 1)

    def rotate(block):
        swapped = jnp.where(
            lane % ROPE < ROPE // 2,
            pltpu.roll(block, 128 - ROPE // 2, 1),
            pltpu.roll(block, ROPE // 2, 1),
        )
        return block * cosine + swapped * sine

    down = project(wa_ref)
    latent = normalize(down[:, :LATENT], lgain_ref[...]).astype(jnp.bfloat16)
    key_rope = rotate(down[:, LATENT:]).astype(jnp.bfloat16)
    key_val = dot32(latent, up_ref[...]).astype(jnp.bfloat16)
    here = pl.ds(pl.multiple_of(tile * TILE, TILE), TILE)
    for head in range(heads):
        k_ref[head, here, :NOPE] = key_val[:, 2 * head * NOPE : (2 * head + 1) * NOPE]
        k_ref[head, here, NOPE:] = key_rope
        v_ref[head, here, :] = key_val[:, (2 * head + 1) * NOPE : (2 * head + 2) * NOPE]

    queries = project(wq_ref)
    nope = queries[:, : heads * NOPE].astype(jnp.bfloat16)
    query = []
    for head in range(heads):
        base = heads * NOPE + (head // 2) * 128
        turned = rotate(queries[:, base : base + 128])
        mine = jnp.where(lane // ROPE == head % 2, turned, 0.0).astype(jnp.bfloat16)
        query.append(jnp.concatenate([nope[:, head * NOPE : (head + 1) * NOPE], mine], axis=1))

    live = live_ref[prompt]
    scale = (NOPE + ROPE) ** (-0.5)
    for count in range(1, LEN // TILE + 1):

        @pl.when(tile == count - 1)
        def _():
            span = count * TILE
            i = lax.broadcasted_iota(jnp.int32, (TILE, span), 0) + (count - 1) * TILE
            j = lax.broadcasted_iota(jnp.int32, (TILE, span), 1)
            allowed = (j <= i) & (j < live)
            for head in range(heads):
                score = lax.dot_general(
                    query[head], k_ref[head, :span, :], (((1,), (1,)), ((), ())),
                    preferred_element_type=jnp.float32,
                )
                score = jnp.where(allowed, score * scale, -1e30)
                expo = jnp.exp(score - jnp.max(score, axis=-1, keepdims=True))
                prob = expo * (1.0 / jnp.sum(expo, axis=-1, keepdims=True))
                out = dot32(prob.astype(jnp.bfloat16), v_ref[head, :span, :])
                o_ref[0, :, head * NOPE : (head + 1) * NOPE] = out.astype(jnp.bfloat16)


def attend(groups, inverse, live, x, again, lgain, cosine, sine, wq, wa, wb):
    per_grp, _, width = x.shape
    heads = wb.shape[1] // (2 * NOPE)
    whole = lambda a: pl.BlockSpec(a.shape, lambda p, t: (0,) * a.ndim)
    smem = pl.BlockSpec(memory_space=pltpu.SMEM)
    return pl.pallas_call(
        functools.partial(layer_kernel, groups, heads),
        grid=(per_grp, LEN // TILE),
        in_specs=[
            smem,
            smem,
            pl.BlockSpec((1, TILE, width), lambda p, t: (p, t, 0)),
            whole(again),
            whole(lgain),
            pl.BlockSpec((TILE, 128), lambda p, t: (t, 0)),
            pl.BlockSpec((TILE, 128), lambda p, t: (t, 0)),
            whole(wq),
            whole(wa),
            whole(wb),
        ],
        out_specs=pl.BlockSpec((1, TILE, heads * NOPE), lambda p, t: (p, t, 0)),
        out_shape=jax.ShapeDtypeStruct((per_grp, LEN, heads * NOPE), jnp.bfloat16),
        scratch_shapes=[
            pltpu.VMEM((TILE, width), jnp.bfloat16),
            pltpu.VMEM(wb.shape, jnp.bfloat16),
            pltpu.VMEM((heads, LEN, 2 * NOPE), jnp.bfloat16),
            pltpu.VMEM((heads, LEN, NOPE), jnp.bfloat16),
        ],
        compiler_params=pltpu.CompilerParams(vmem_limit_bytes=48 * 1024 * 1024),
        cost_estimate=pl.CostEstimate(
            flops=20_000_000_000, bytes_accessed=16_000_000, transcendentals=4_000_000
        ),
    )(inverse, live, x, again, lgain, cosine, sine, wq, wa, wb)


def rotate_half(values, position):
    half_dim = values.shape[-1] // 2
    frequency = 10000.0 ** (-jnp.arange(half_dim, dtype=jnp.float32) / half_dim)
    angles = position.astype(jnp.float32)[..., None] * frequency
    cosine = jnp.cos(angles)
    sine = jnp.sin(angles)
    first_half = values[..., :half_dim]
    second_half = values[..., half_dim:]
    return jnp.concatenate(
        [first_half * cosine - second_half * sine, first_half * sine + second_half * cosine],
        axis=-1,
    )


def split_positions(
    inputs, inverse, live_len, attn_gain, latent_gain, w_query, w_down_kv, w_up_kv, w_out
):
    groups = lax.axis_size("dp")

    def arrange(gathered):
        block_rows = gathered.shape[0] // groups
        blocks = gathered.reshape((groups, block_rows) + gathered.shape[1:])
        return jnp.take(blocks, inverse, axis=0).reshape(gathered.shape)

    query_w, down_w, up_w, out_w = (
        lax.all_gather(w_query.astype(jnp.bfloat16), "dp", axis=0, tiled=True),
        lax.all_gather(w_down_kv.astype(jnp.bfloat16), "dp", axis=0, tiled=True),
        lax.all_gather(w_up_kv.astype(jnp.bfloat16), "dp", axis=0, tiled=True),
        lax.all_gather(w_out.astype(jnp.bfloat16), "dp", axis=0, tiled=True),
    )
    query_w = arrange(query_w)
    down_w = arrange(down_w)
    up_w = arrange(up_w)
    out_w = arrange(out_w)
    query_w, up_w = (
        lax.all_gather(query_w, "ty", axis=1, tiled=True),
        lax.all_gather(up_w, "ty", axis=1, tiled=True),
    )
    per_grp, quarter, width = inputs.shape
    heads = query_w.shape[1] // (NOPE + ROPE)
    position = lax.axis_index("ty") * quarter + jnp.arange(quarter, dtype=jnp.int32)
    flat_rows = inputs.reshape(per_grp * quarter, width)
    normed = normalize(flat_rows, attn_gain).astype(jnp.bfloat16)
    queries = jnp.dot(normed, query_w, preferred_element_type=jnp.float32).reshape(
        per_grp, quarter, heads, NOPE + ROPE
    )
    queries = jnp.concatenate(
        [queries[..., :NOPE], rotate_half(queries[..., NOPE:], position[None, :, None])], axis=-1
    ).astype(jnp.bfloat16)
    down_proj = jnp.dot(normed, down_w, preferred_element_type=jnp.float32).reshape(
        per_grp, quarter, LATENT + ROPE
    )
    latent = normalize(down_proj[..., :LATENT], latent_gain).astype(jnp.bfloat16)
    key_rope = rotate_half(down_proj[..., LATENT:], position[None, :]).astype(jnp.bfloat16)
    gathered = lax.all_gather(
        jnp.concatenate([latent, key_rope], axis=-1), "ty", axis=1, tiled=True
    )
    key_val = jnp.dot(gathered[..., :LATENT], up_w, preferred_element_type=jnp.float32).astype(
        jnp.bfloat16
    )
    rope_all = gathered[..., LATENT:]
    key_val = key_val.reshape(per_grp, LEN, heads, 2, NOPE)
    key_nope = key_val[:, :, :, 0]
    values = key_val[:, :, :, 1]
    score_scale = (NOPE + ROPE) ** (-0.5)
    scores = (
        jnp.einsum(
            "pqhd,pkhd->phqk", queries[..., :NOPE], key_nope, preferred_element_type=jnp.float32
        )
        + jnp.einsum(
            "pqhd,pkd->phqk", queries[..., NOPE:], rope_all, preferred_element_type=jnp.float32
        )
    ) * score_scale
    key_pos = jnp.arange(LEN, dtype=jnp.int32)
    allowed = (key_pos[None, None, :] <= position[None, :, None]) & (
        key_pos[None, None, :] < live_len[:, None, None]
    )
    scores = jnp.where(allowed[:, None], scores, -1e30)
    top = jnp.max(scores, axis=-1, keepdims=True)
    expo = jnp.exp(scores - top)
    softmax_w = (expo / jnp.sum(expo, axis=-1, keepdims=True)).astype(jnp.bfloat16)
    attended = jnp.einsum(
        "phqk,pkhd->pqhd", softmax_w, values, preferred_element_type=jnp.float32
    ).astype(jnp.bfloat16)
    attended = attended.reshape(per_grp * quarter, heads * NOPE)
    own_width = width // lax.axis_size("tx")
    col_start = lax.axis_index("tx") * own_width
    partial_value = lax.dot_general(
        attended, out_w, (((1,), (1,)), ((), ())), preferred_element_type=jnp.float32
    ).reshape(per_grp, quarter, width)
    summed = lax.psum_scatter(partial_value, "tx", scatter_dimension=2, tiled=True)
    residual = lax.dynamic_slice_in_dim(inputs, col_start, own_width, 2)
    layer_out = (residual.astype(jnp.float32) + summed).astype(jnp.bfloat16)
    return layer_out


def split_heads(
    inputs, inverse, live_len, attn_gain, latent_gain, w_query, w_down_kv, w_up_kv, w_out
):
    groups = lax.axis_size("dp")
    tx_size, ty_size = lax.axis_size("tx"), lax.axis_size("ty")
    tx, ty = lax.axis_index("tx"), lax.axis_index("ty")
    per_grp, quarter, width = inputs.shape
    half = width // tx_size
    rows = w_query.shape[0]
    heads = w_query.shape[1] // (NOPE + ROPE)
    wq = w_query.astype(jnp.bfloat16).reshape(rows, heads, NOPE + ROPE)
    rope_q = wq[:, :, NOPE:].reshape(rows, heads * ROPE)
    rope_q = jnp.pad(rope_q, ((0, 0), (0, -(heads * ROPE) % 128)))
    wq = jnp.concatenate([wq[:, :, :NOPE].reshape(rows, heads * NOPE), rope_q], axis=1)
    wa = w_down_kv.astype(jnp.bfloat16)

    x_all = lax.all_gather(inputs, "ty", axis=1, tiled=True)
    wa = lax.all_gather(wa, "dp", axis=0, tiled=True)
    wa = jnp.concatenate([wa, wa[:, LATENT:]], axis=1)
    wq = lax.all_gather(wq, "dp", axis=0, tiled=True)
    wb = lax.all_gather(w_up_kv.astype(jnp.bfloat16), "dp", axis=0, tiled=True)

    position = jnp.arange(LEN, dtype=jnp.float32)
    frequency = 10000.0 ** (-jnp.arange(ROPE // 2, dtype=jnp.float32) / (ROPE // 2))
    angles = position[:, None] * frequency
    cosine, sine = jnp.cos(angles), jnp.sin(angles)
    cosine = jnp.concatenate([cosine] * 4, axis=1)
    sine = jnp.concatenate([-sine, sine, -sine, sine], axis=1)

    mixed = attend(
        groups, inverse, live_len, x_all, attn_gain[None], latent_gain[None], cosine, sine,
        wq, wa, wb,
    )

    piece = w_out.shape[1] // ty_size
    wo = lax.dynamic_slice_in_dim(w_out, ty * piece, piece, 1).astype(jnp.bfloat16)
    wo = lax.all_gather(wo, "dp", axis=0, tiled=False)
    wo = jnp.take(wo, inverse, axis=0).reshape(tx_size, half, piece)
    wo = lax.all_to_all(wo, "tx", split_axis=0, concat_axis=0, tiled=True)
    wo = lax.all_gather(wo, "ty", axis=1, tiled=False)

    spread = mixed.reshape(per_grp, ty_size, quarter, heads * NOPE)
    spread = jnp.moveaxis(spread, 1, 0)
    spread = lax.all_to_all(spread, "ty", split_axis=0, concat_axis=0, tiled=True)
    spread = lax.all_gather(spread, "tx", axis=0, tiled=False)
    branch = lax.dot_general(
        jnp.moveaxis(spread.reshape(tx_size * ty_size, per_grp * quarter, -1), 0, 1).reshape(
            per_grp * quarter, -1
        ),
        jnp.moveaxis(wo.reshape(tx_size * ty_size, half, piece), 0, 1).reshape(half, -1),
        (((1,), (1,)), ((), ())),
        preferred_element_type=jnp.float32,
    ).reshape(per_grp, quarter, half)
    residual = lax.dynamic_slice_in_dim(inputs, tx * half, half, 2)
    layer_out = (residual.astype(jnp.float32) + branch).astype(jnp.bfloat16)
    return layer_out


def shards(
    inputs,
    lengths,
    prompt_deal,
    block_owner,
    attn_gain,
    latent_gain,
    final_gain,
    w_query,
    w_down_kv,
    w_up_kv,
    w_out,
    w_vocab,
):
    groups = lax.axis_size("dp")
    dp, tx, ty = lax.axis_index("dp"), lax.axis_index("tx"), lax.axis_index("ty")
    per_grp, quarter, width = inputs.shape
    half = width // lax.axis_size("tx")
    order = jnp.arange(groups, dtype=jnp.int32)
    inverse = jnp.sum(
        jnp.where(block_owner[None, :] == order[:, None], order[None, :], 0), axis=1
    ).astype(jnp.int32)
    slots = dp * per_grp + jnp.arange(per_grp, dtype=jnp.int32)
    live_len = jnp.take(lengths, jnp.take(prompt_deal, slots))

    rows = w_query.shape[0]
    layer = split_positions if w_query.shape[1] % (NOPE + ROPE) else split_heads
    layer_out = layer(
        inputs, inverse, live_len, attn_gain, latent_gain, w_query, w_down_kv, w_up_kv, w_out
    )

    at = live_len - 1 - ty * quarter
    picked = jnp.stack(
        [
            lax.dynamic_slice(
                layer_out, (i, jnp.clip(at[i], 0, quarter - 1), 0), (1, 1, half)
            ).reshape(half)
            for i in range(per_grp)
        ]
    ).astype(jnp.float32)
    inside = (at >= 0) & (at < quarter)
    picked = jnp.where(inside[:, None], picked, 0.0)
    placed = lax.dynamic_update_slice(
        jnp.zeros((groups * per_grp, width), jnp.float32), picked, (dp * per_grp, tx * half)
    )
    last_rows = lax.psum(placed, ("dp", "tx", "ty"))
    final_rows = normalize(last_rows, final_gain).astype(jnp.bfloat16)
    mine = lax.dynamic_slice_in_dim(final_rows, block_owner[dp] * rows, rows, 1)
    partial = dot32(mine, w_vocab.astype(jnp.bfloat16))
    logits = lax.psum_scatter(partial, "dp", scatter_dimension=0, tiled=True)
    return (layer_out, logits)


def solution(mesh):
    placed = (
        P("dp", "ty", None),
        P(),
        P(),
        P(),
        P(),
        P(),
        P(),
        P("dp", ("tx", "ty")),
        P("dp", None),
        P("dp", ("tx", "ty")),
        P("dp", "tx"),
        P("dp", ("tx", "ty")),
    )
    return jax.shard_map(
        shards,
        mesh=mesh,
        in_specs=placed,
        out_specs=(P("dp", "ty", "tx"), P("dp", ("tx", "ty"))),
        check_vma=False,
    )
```

```python
import functools

import jax
import jax.numpy as jnp
from jax import lax
from jax.experimental import pallas as pl
from jax.experimental.pallas import tpu as pltpu
from jax.sharding import PartitionSpec as P

NOPE = 128
ROPE = 64
LATENT = 512
LEN = 1024
TILE = 256
EPS = 1e-06


def normalize(values, gain):
    wide = values.astype(jnp.float32)
    return wide * lax.rsqrt(jnp.mean(wide * wide, axis=-1, keepdims=True) + EPS) * gain


def dot32(left, right):
    return jnp.dot(left, right, preferred_element_type=jnp.float32)


def remote(src, dst, send, recv, **where):
    return pltpu.make_async_remote_copy(
        src_ref=src,
        dst_ref=dst,
        send_sem=send,
        recv_sem=recv,
        device_id=where,
        device_id_type=pl.DeviceIdType.MESH,
    )


def greet(**where):
    pl.semaphore_signal(
        pltpu.get_barrier_semaphore(),
        inc=1,
        device_id=where,
        device_id_type=pl.DeviceIdType.MESH,
    )


def gather_kernel(
    groups, chunks, x_ref, wq_ref, wa_ref, wb_ref, wo_ref, xs_ref, wqs_ref, was_ref, wbs_ref,
    wos_ref, z_send, z_recv, x_send, x_recv, y_send, y_recv, p_send, p_recv, a_send, a_recv,
    local,
):
    dp, tx, ty = lax.axis_index("dp"), lax.axis_index("tx"), lax.axis_index("ty")
    core = ty % 2
    partner = ty + 1 - 2 * core
    across = (ty + 2) % 4
    other = 1 - tx
    rows = x_ref.shape[1] // chunks
    steps = groups - 1

    greet(ty=partner)
    greet(ty=across)
    greet(tx=other)
    barrier = pltpu.get_barrier_semaphore()

    @pl.when(dp > 0)
    def _():
        greet(dp=dp - 1)

    @pl.when(dp < groups - 1)
    def _():
        greet(dp=dp + 1)

    ends = (dp > 0).astype(jnp.int32) + (dp < groups - 1).astype(jnp.int32)
    pl.semaphore_wait(barrier, 3 + ends)

    tensors = [
        (wq_ref, lambda g: wqs_ref.at[g]),
        (wa_ref, lambda g: was_ref.at[g, core]),
        (wb_ref, lambda g: wbs_ref.at[g]),
        (wo_ref, lambda g: wos_ref.at[g]),
    ]

    def hop(which, way, step):
        own, slot = tensors[which]
        sign = 1 - 2 * way
        block = dp - sign * step
        runs = (block >= 0) & (block < groups) & (dp + sign >= 0) & (dp + sign < groups)
        source = own if step == 0 else slot(block)
        copy = remote(
            source, slot(block), z_send.at[way, which, step], z_recv.at[way, which, step],
            dp=dp + sign,
        )
        return copy, runs

    def arrival(which, way, step):
        own, slot = tensors[which]
        sign = 1 - 2 * way
        block = dp - sign * (step + 1)
        copy = remote(
            own, slot(block), z_send.at[way, which, step], z_recv.at[way, which, step], dp=dp
        )
        return copy, (block >= 0) & (block < groups)

    def start_hop(which, step):
        for way in range(2):
            copy, runs = hop(which, way, step)
            pl.when(runs)(copy.start)

    def wait_hop(which, step):
        for way in range(2):
            copy, comes = arrival(which, way, step)
            pl.when(comes)(copy.wait_recv)

    def cut(ref, slot, prompt, k):
        return ref.at[slot, prompt, pl.ds(k * rows, rows)]

    def crossing(k, slot):
        src = x_ref.at[tx, pl.ds(k * rows, rows)]
        return remote(src, cut(xs_ref, slot, tx, k), x_send.at[k], x_recv.at[k], ty=across)

    def sideways(k, prompt):
        part = cut(xs_ref, across, prompt, k)
        return remote(part, part, y_send.at[k], y_recv.at[k], tx=other)

    def inward(k, half, slot, prompt):
        part = cut(xs_ref, slot, prompt, k)
        return remote(part, part, p_send.at[half, k], p_recv.at[half, k], ty=partner)

    def own_block(slot):
        return remote(x_ref, xs_ref.at[slot], a_send.at[0], a_recv.at[0], ty=partner)

    def down_half(side):
        part = was_ref.at[:, side]
        return remote(part, part, a_send.at[1], a_recv.at[1], ty=partner)

    for k in range(chunks):
        crossing(k, ty).start()
        if k < len(tensors):
            start_hop(k, 0)
    own_block(ty).start()
    mine = [pltpu.make_async_copy(x_ref, xs_ref.at[ty], local.at[len(tensors)])]
    for which, (own, slot) in enumerate(tensors):
        mine.append(pltpu.make_async_copy(own, slot(dp), local.at[which]))
    for copy in mine:
        copy.start()

    for k in range(chunks):
        crossing(k, across).wait_recv()
        sideways(k, tx).start()
        inward(k, 0, across, tx).start()
        if k < len(tensors):
            wait_hop(k, 0)
            if steps > 1:
                start_hop(k, 1)
    for k in range(chunks):
        sideways(k, other).wait_recv()
        inward(k, 1, across, other).start()
    for step in range(1, steps):
        for which in range(len(tensors)):
            wait_hop(which, step)
            if step + 1 < steps:
                start_hop(which, step + 1)
            if step == steps - 1 and which == 1:
                mine[2].wait()
                down_half(core).start()

    mine[0].wait()
    mine[1].wait()
    mine[3].wait()
    mine[4].wait()
    down_half(1 - core).wait_recv()
    own_block(partner).wait_recv()
    far = (partner + 2) % 4
    for k in range(chunks):
        inward(k, 0, far, tx).wait_recv()
        inward(k, 1, far, other).wait_recv()
    for step in range(steps):
        for which in range(len(tensors)):
            for way in range(2):
                copy, runs = hop(which, way, step)
                pl.when(runs)(copy.wait_send)
    for k in range(chunks):
        crossing(k, ty).wait_send()
        sideways(k, tx).wait_send()
        inward(k, 0, across, tx).wait_send()
        inward(k, 1, across, other).wait_send()
    own_block(ty).wait_send()
    down_half(core).wait_send()


def gather_all(groups, x, wq, wa, wb, wo):
    chunks = 4
    steps = max(groups - 1, 1)
    shape = lambda *dims: jax.ShapeDtypeStruct(dims, jnp.bfloat16)
    dma = pltpu.SemaphoreType.DMA
    return pl.pallas_call(
        functools.partial(gather_kernel, groups, chunks),
        in_specs=[pl.BlockSpec(memory_space=pl.ANY)] * 5,
        out_specs=[pl.BlockSpec(memory_space=pl.ANY)] * 5,
        out_shape=[
            shape(4, *x.shape),
            shape(groups, *wq.shape),
            shape(groups, 2, *wa.shape),
            shape(groups, *wb.shape),
            shape(groups, *wo.shape),
        ],
        scratch_shapes=[
            dma((2, 4, steps)), dma((2, 4, steps)),
            dma((chunks,)), dma((chunks,)), dma((chunks,)), dma((chunks,)),
            dma((2, chunks)), dma((2, chunks)), dma((2,)), dma((2,)), dma((5,)),
        ],
        compiler_params=pltpu.CompilerParams(collective_id=0, has_side_effects=True),
        cost_estimate=pl.CostEstimate(flops=0, bytes_accessed=100_000_000, transcendentals=0),
    )(x, wq, wa, wb, wo)


def tail_kernel(
    groups, tx_size, ty_size, vocab_chunk, owner_ref, picked_ref, gain_ref, vocab_ref, out_ref,
    seen, full, rows_ref, table, part, incoming, t_send, t_recv, r_send, r_recv, l_send, l_recv,
    v_sem,
):
    dp, tx, ty = lax.axis_index("dp"), lax.axis_index("tx"), lax.axis_index("ty")
    per_grp, half = picked_ref.shape
    block = table.shape[0]
    peers = groups * tx_size
    place = dp * tx_size + tx
    count = vocab_ref.shape[1] // vocab_chunk

    loads = []
    for k in range(count):
        cols = pl.ds(k * vocab_chunk, vocab_chunk)
        loads.append(
            pltpu.make_async_copy(vocab_ref.at[:, cols], table.at[:, cols], v_sem.at[k])
        )
        loads[-1].start()

    for k in range(1, ty_size):
        greet(ty=(ty + k) % ty_size)
    for k in range(1, peers):
        peer = (place + k) % peers
        greet(dp=peer // tx_size, tx=peer % tx_size)
    pl.semaphore_wait(pltpu.get_barrier_semaphore(), ty_size + peers - 2)

    def along_ty(k, slot):
        return remote(
            picked_ref, seen.at[slot], t_send.at[k], t_recv.at[k], ty=(ty + k) % ty_size
        )

    for k in range(1, ty_size):
        along_ty(k, ty).start()
    merged = picked_ref[...]
    for k in range(1, ty_size):
        slot = (ty + ty_size - k) % ty_size
        along_ty(k, slot).wait_recv()
        merged = merged + seen[slot]
    full[place] = merged

    def along_peers(k, slot):
        peer = (place + k) % peers
        return remote(
            full.at[place], full.at[slot], r_send.at[k], r_recv.at[k],
            dp=peer // tx_size, tx=peer % tx_size,
        )

    for k in range(1, peers):
        along_peers(k, place).start()
    for k in range(1, peers):
        along_peers(k, (place + peers - k) % peers).wait_recv()
    for g in range(groups):
        for t in range(tx_size):
            rows_ref[g * per_grp : (g + 1) * per_grp, t * half : (t + 1) * half] = full[
                g * tx_size + t
            ]
    final = normalize(rows_ref[...], gain_ref[...])
    owner = owner_ref[dp]
    mine = jnp.zeros((groups * per_grp, block), jnp.float32)
    for g in range(groups):
        mine = jnp.where(owner == g, final[:, g * block : (g + 1) * block], mine)
    mine = mine.astype(jnp.bfloat16)
    for k in range(count):
        loads[k].wait()
        cols = slice(k * vocab_chunk, (k + 1) * vocab_chunk)
        logits = dot32(mine, table[:, cols].astype(jnp.bfloat16))
        for g in range(groups):
            part[g, :, cols] = logits[g * per_grp : (g + 1) * per_grp]

    def along_dp(k, slot):
        peer = (dp + k) % groups
        return remote(part.at[peer], incoming.at[slot], l_send.at[k], l_recv.at[k], dp=peer)

    for k in range(1, groups):
        along_dp(k, dp).start()
    total = part[dp]
    for k in range(1, groups):
        slot = (dp + groups - k) % groups
        along_dp(k, slot).wait_recv()
        total = total + incoming[slot]
    out_ref[...] = total
    for k in range(1, ty_size):
        along_ty(k, ty).wait_send()
    for k in range(1, peers):
        along_peers(k, place).wait_send()
    for k in range(1, groups):
        along_dp(k, dp).wait_send()


def tail(groups, tx_size, ty_size, owner, picked, gain, vocab):
    per_grp, half = picked.shape
    block, words = vocab.shape
    vocab_chunk = 512
    peers = groups * tx_size
    dma = pltpu.SemaphoreType.DMA
    vmem = pl.BlockSpec(memory_space=pltpu.VMEM)
    return pl.pallas_call(
        functools.partial(tail_kernel, groups, tx_size, ty_size, vocab_chunk),
        in_specs=[
            pl.BlockSpec(memory_space=pltpu.SMEM), vmem, vmem, pl.BlockSpec(memory_space=pl.ANY),
        ],
        out_specs=vmem,
        out_shape=jax.ShapeDtypeStruct((per_grp, words), jnp.float32),
        scratch_shapes=[
            pltpu.VMEM((ty_size, per_grp, half), jnp.float32),
            pltpu.VMEM((peers, per_grp, half), jnp.float32),
            pltpu.VMEM((groups * per_grp, half * tx_size), jnp.float32),
            pltpu.VMEM((block, words), jnp.float32),
            pltpu.VMEM((groups, per_grp, words), jnp.float32),
            pltpu.VMEM((groups, per_grp, words), jnp.float32),
            dma((ty_size,)), dma((ty_size,)), dma((peers,)), dma((peers,)),
            dma((groups,)), dma((groups,)), dma((words // vocab_chunk,)),
        ],
        compiler_params=pltpu.CompilerParams(
            collective_id=1, has_side_effects=True, vmem_limit_bytes=40 * 1024 * 1024
        ),
        cost_estimate=pl.CostEstimate(
            flops=100_000_000, bytes_accessed=16_000_000, transcendentals=0
        ),
    )(owner, picked, gain, vocab)


def layer_kernel(
    groups, heads, inv_ref, live_ref, x_ref, again_ref, lgain_ref, cos_ref, sin_ref,
    wq_ref, wa_ref, wb_ref, o_ref, h_ref, up_ref, k_ref, v_ref,
):
    prompt, tile = pl.program_id(0), pl.program_id(1)
    width = x_ref.shape[-1]
    rows = width // groups
    up_rows = LATENT // groups

    @pl.when((prompt == 0) & (tile == 0))
    def _():
        for g in range(groups):
            start = pl.multiple_of(inv_ref[g] * up_rows, up_rows)
            up_ref[g * up_rows : (g + 1) * up_rows, :] = wb_ref[pl.ds(start, up_rows), :]

    h_ref[...] = normalize(x_ref[0, 0], again_ref[...]).astype(jnp.bfloat16)

    def project(w_ref):
        total = None
        for g in range(groups):
            start = pl.multiple_of(inv_ref[g] * rows, rows)
            part = dot32(h_ref[:, g * rows : (g + 1) * rows], w_ref[pl.ds(start, rows), :])
            total = part if total is None else total + part
        return total

    cosine, sine = cos_ref[...], sin_ref[...]
    lane = lax.broadcasted_iota(jnp.int32, (TILE, 128), 1)

    def rotate(block):
        swapped = jnp.where(
            lane % ROPE < ROPE // 2,
            pltpu.roll(block, 128 - ROPE // 2, 1),
            pltpu.roll(block, ROPE // 2, 1),
        )
        return block * cosine + swapped * sine

    down = project(wa_ref)
    latent = normalize(down[:, :LATENT], lgain_ref[...]).astype(jnp.bfloat16)
    key_rope = rotate(down[:, LATENT:]).astype(jnp.bfloat16)
    key_val = dot32(latent, up_ref[...]).astype(jnp.bfloat16)
    here = pl.ds(pl.multiple_of(tile * TILE, TILE), TILE)
    for head in range(heads):
        k_ref[head, here, :NOPE] = key_val[:, 2 * head * NOPE : (2 * head + 1) * NOPE]
        k_ref[head, here, NOPE:] = key_rope
        v_ref[head, here, :] = key_val[:, (2 * head + 1) * NOPE : (2 * head + 2) * NOPE]

    queries = project(wq_ref)
    nope = queries[:, : heads * NOPE].astype(jnp.bfloat16)
    query = []
    for head in range(heads):
        base = heads * NOPE + (head // 2) * 128
        turned = rotate(queries[:, base : base + 128])
        mine = jnp.where(lane // ROPE == head % 2, turned, 0.0).astype(jnp.bfloat16)
        query.append(jnp.concatenate([nope[:, head * NOPE : (head + 1) * NOPE], mine], axis=1))

    live = live_ref[prompt]
    scale = (NOPE + ROPE) ** (-0.5)
    for count in range(1, LEN // TILE + 1):

        @pl.when(tile == count - 1)
        def _():
            span = count * TILE
            i = lax.broadcasted_iota(jnp.int32, (TILE, span), 0) + (count - 1) * TILE
            j = lax.broadcasted_iota(jnp.int32, (TILE, span), 1)
            allowed = (j <= i) & (j < live)
            for head in range(heads):
                score = lax.dot_general(
                    query[head], k_ref[head, :span, :], (((1,), (1,)), ((), ())),
                    preferred_element_type=jnp.float32,
                )
                score = jnp.where(allowed, score * scale, -1e30)
                expo = jnp.exp(score - jnp.max(score, axis=-1, keepdims=True))
                prob = expo * (1.0 / jnp.sum(expo, axis=-1, keepdims=True))
                out = dot32(prob.astype(jnp.bfloat16), v_ref[head, :span, :])
                o_ref[0, :, head * NOPE : (head + 1) * NOPE] = out.astype(jnp.bfloat16)


def attend(groups, inverse, live, x, again, lgain, cosine, sine, wq, wa, wb):
    _, per_grp, _, width = x.shape
    heads = wb.shape[1] // (2 * NOPE)
    whole = lambda a: pl.BlockSpec(a.shape, lambda p, t: (0,) * a.ndim)
    smem = pl.BlockSpec(memory_space=pltpu.SMEM)
    return pl.pallas_call(
        functools.partial(layer_kernel, groups, heads),
        grid=(per_grp, LEN // TILE),
        in_specs=[
            smem,
            smem,
            pl.BlockSpec((1, 1, TILE, width), lambda p, t: (t, p, 0, 0)),
            whole(again),
            whole(lgain),
            pl.BlockSpec((TILE, 128), lambda p, t: (t, 0)),
            pl.BlockSpec((TILE, 128), lambda p, t: (t, 0)),
            whole(wq),
            whole(wa),
            whole(wb),
        ],
        out_specs=pl.BlockSpec((1, TILE, heads * NOPE), lambda p, t: (p, t, 0)),
        out_shape=jax.ShapeDtypeStruct((per_grp, LEN, heads * NOPE), jnp.bfloat16),
        scratch_shapes=[
            pltpu.VMEM((TILE, width), jnp.bfloat16),
            pltpu.VMEM(wb.shape, jnp.bfloat16),
            pltpu.VMEM((heads, LEN, 2 * NOPE), jnp.bfloat16),
            pltpu.VMEM((heads, LEN, NOPE), jnp.bfloat16),
        ],
        compiler_params=pltpu.CompilerParams(vmem_limit_bytes=48 * 1024 * 1024),
        cost_estimate=pl.CostEstimate(
            flops=20_000_000_000, bytes_accessed=16_000_000, transcendentals=4_000_000
        ),
    )(inverse, live, x, again, lgain, cosine, sine, wq, wa, wb)


def rotate_half(values, position):
    half_dim = values.shape[-1] // 2
    frequency = 10000.0 ** (-jnp.arange(half_dim, dtype=jnp.float32) / half_dim)
    angles = position.astype(jnp.float32)[..., None] * frequency
    cosine = jnp.cos(angles)
    sine = jnp.sin(angles)
    first_half = values[..., :half_dim]
    second_half = values[..., half_dim:]
    return jnp.concatenate(
        [first_half * cosine - second_half * sine, first_half * sine + second_half * cosine],
        axis=-1,
    )


def split_positions(
    inputs, inverse, live_len, attn_gain, latent_gain, w_query, w_down_kv, w_up_kv, w_out
):
    groups = lax.axis_size("dp")

    def arrange(gathered):
        block_rows = gathered.shape[0] // groups
        blocks = gathered.reshape((groups, block_rows) + gathered.shape[1:])
        return jnp.take(blocks, inverse, axis=0).reshape(gathered.shape)

    query_w, down_w, up_w, out_w = (
        lax.all_gather(w_query.astype(jnp.bfloat16), "dp", axis=0, tiled=True),
        lax.all_gather(w_down_kv.astype(jnp.bfloat16), "dp", axis=0, tiled=True),
        lax.all_gather(w_up_kv.astype(jnp.bfloat16), "dp", axis=0, tiled=True),
        lax.all_gather(w_out.astype(jnp.bfloat16), "dp", axis=0, tiled=True),
    )
    query_w = arrange(query_w)
    down_w = arrange(down_w)
    up_w = arrange(up_w)
    out_w = arrange(out_w)
    query_w, up_w = (
        lax.all_gather(query_w, "ty", axis=1, tiled=True),
        lax.all_gather(up_w, "ty", axis=1, tiled=True),
    )
    per_grp, quarter, width = inputs.shape
    heads = query_w.shape[1] // (NOPE + ROPE)
    position = lax.axis_index("ty") * quarter + jnp.arange(quarter, dtype=jnp.int32)
    flat_rows = inputs.reshape(per_grp * quarter, width)
    normed = normalize(flat_rows, attn_gain).astype(jnp.bfloat16)
    queries = jnp.dot(normed, query_w, preferred_element_type=jnp.float32).reshape(
        per_grp, quarter, heads, NOPE + ROPE
    )
    queries = jnp.concatenate(
        [queries[..., :NOPE], rotate_half(queries[..., NOPE:], position[None, :, None])], axis=-1
    ).astype(jnp.bfloat16)
    down_proj = jnp.dot(normed, down_w, preferred_element_type=jnp.float32).reshape(
        per_grp, quarter, LATENT + ROPE
    )
    latent = normalize(down_proj[..., :LATENT], latent_gain).astype(jnp.bfloat16)
    key_rope = rotate_half(down_proj[..., LATENT:], position[None, :]).astype(jnp.bfloat16)
    gathered = lax.all_gather(
        jnp.concatenate([latent, key_rope], axis=-1), "ty", axis=1, tiled=True
    )
    key_val = jnp.dot(gathered[..., :LATENT], up_w, preferred_element_type=jnp.float32).astype(
        jnp.bfloat16
    )
    rope_all = gathered[..., LATENT:]
    key_val = key_val.reshape(per_grp, LEN, heads, 2, NOPE)
    key_nope = key_val[:, :, :, 0]
    values = key_val[:, :, :, 1]
    score_scale = (NOPE + ROPE) ** (-0.5)
    scores = (
        jnp.einsum(
            "pqhd,pkhd->phqk", queries[..., :NOPE], key_nope, preferred_element_type=jnp.float32
        )
        + jnp.einsum(
            "pqhd,pkd->phqk", queries[..., NOPE:], rope_all, preferred_element_type=jnp.float32
        )
    ) * score_scale
    key_pos = jnp.arange(LEN, dtype=jnp.int32)
    allowed = (key_pos[None, None, :] <= position[None, :, None]) & (
        key_pos[None, None, :] < live_len[:, None, None]
    )
    scores = jnp.where(allowed[:, None], scores, -1e30)
    top = jnp.max(scores, axis=-1, keepdims=True)
    expo = jnp.exp(scores - top)
    softmax_w = (expo / jnp.sum(expo, axis=-1, keepdims=True)).astype(jnp.bfloat16)
    attended = jnp.einsum(
        "phqk,pkhd->pqhd", softmax_w, values, preferred_element_type=jnp.float32
    ).astype(jnp.bfloat16)
    attended = attended.reshape(per_grp * quarter, heads * NOPE)
    own_width = width // lax.axis_size("tx")
    col_start = lax.axis_index("tx") * own_width
    partial_value = lax.dot_general(
        attended, out_w, (((1,), (1,)), ((), ())), preferred_element_type=jnp.float32
    ).reshape(per_grp, quarter, width)
    summed = lax.psum_scatter(partial_value, "tx", scatter_dimension=2, tiled=True)
    residual = lax.dynamic_slice_in_dim(inputs, col_start, own_width, 2)
    layer_out = (residual.astype(jnp.float32) + summed).astype(jnp.bfloat16)
    return layer_out


def split_heads(
    inputs, inverse, live_len, attn_gain, latent_gain, w_query, w_down_kv, w_up_kv, w_out
):
    groups = lax.axis_size("dp")
    tx_size, ty_size = lax.axis_size("tx"), lax.axis_size("ty")
    tx, ty = lax.axis_index("tx"), lax.axis_index("ty")
    per_grp, quarter, width = inputs.shape
    half = width // tx_size
    rows = w_query.shape[0]
    heads = w_query.shape[1] // (NOPE + ROPE)
    wq = w_query.astype(jnp.bfloat16).reshape(rows, heads, NOPE + ROPE)
    rope_q = wq[:, :, NOPE:].reshape(rows, heads * ROPE)
    rope_q = jnp.pad(rope_q, ((0, 0), (0, -(heads * ROPE) % 128)))
    wq = jnp.concatenate([wq[:, :, :NOPE].reshape(rows, heads * NOPE), rope_q], axis=1)
    wa = lax.dynamic_slice_in_dim(w_down_kv, (ty % 2) * (rows // 2), rows // 2, 0)
    wa = jnp.concatenate([wa, wa[:, LATENT:]], axis=1).astype(jnp.bfloat16)
    piece = w_out.shape[1] // ty_size
    wo = lax.dynamic_slice_in_dim(w_out, ty * piece, piece, 1).astype(jnp.bfloat16)
    x_all, wq, wa, wb, wo = gather_all(
        groups, inputs, wq, wa, w_up_kv.astype(jnp.bfloat16), wo
    )
    wq, wa, wb = (w.reshape(-1, w.shape[-1]) for w in (wq, wa, wb))

    position = jnp.arange(LEN, dtype=jnp.float32)
    frequency = 10000.0 ** (-jnp.arange(ROPE // 2, dtype=jnp.float32) / (ROPE // 2))
    angles = position[:, None] * frequency
    cosine, sine = jnp.cos(angles), jnp.sin(angles)
    cosine = jnp.concatenate([cosine] * 4, axis=1)
    sine = jnp.concatenate([-sine, sine, -sine, sine], axis=1)

    mixed = attend(
        groups, inverse, live_len, x_all, attn_gain[None], latent_gain[None], cosine, sine,
        wq, wa, wb,
    )

    wo = jnp.take(wo, inverse, axis=0).reshape(tx_size, half, piece)
    passed = lax.ppermute(jnp.where(tx == 0, wo[1], wo[0]), "tx", [(0, 1), (1, 0)])
    kept = jnp.where(tx == 0, wo[0], wo[1])
    wo = jnp.where(tx == 0, jnp.stack([kept, passed]), jnp.stack([passed, kept]))
    wo = lax.all_gather(wo, "ty", axis=1, tiled=False)

    spread = mixed.reshape(per_grp, ty_size, quarter, heads * NOPE)
    spread = jnp.moveaxis(spread, 1, 0)
    spread = lax.all_to_all(spread, "ty", split_axis=0, concat_axis=0, tiled=True)
    spread = lax.all_gather(spread, "tx", axis=0, tiled=False)
    branch = lax.dot_general(
        jnp.moveaxis(spread.reshape(tx_size * ty_size, per_grp * quarter, -1), 0, 1).reshape(
            per_grp * quarter, -1
        ),
        jnp.moveaxis(wo.reshape(tx_size * ty_size, half, piece), 0, 1).reshape(half, -1),
        (((1,), (1,)), ((), ())),
        preferred_element_type=jnp.float32,
    ).reshape(per_grp, quarter, half)
    residual = lax.dynamic_slice_in_dim(inputs, tx * half, half, 2)
    layer_out = (residual.astype(jnp.float32) + branch).astype(jnp.bfloat16)
    return layer_out


def shards(
    inputs,
    lengths,
    prompt_deal,
    block_owner,
    attn_gain,
    latent_gain,
    final_gain,
    w_query,
    w_down_kv,
    w_up_kv,
    w_out,
    w_vocab,
):
    groups = lax.axis_size("dp")
    dp, tx, ty = lax.axis_index("dp"), lax.axis_index("tx"), lax.axis_index("ty")
    per_grp, quarter, width = inputs.shape
    half = width // lax.axis_size("tx")
    order = jnp.arange(groups, dtype=jnp.int32)
    inverse = jnp.sum(
        jnp.where(block_owner[None, :] == order[:, None], order[None, :], 0), axis=1
    ).astype(jnp.int32)
    slots = dp * per_grp + jnp.arange(per_grp, dtype=jnp.int32)
    live_len = jnp.take(lengths, jnp.take(prompt_deal, slots))

    whole_heads = w_query.shape[1] % (NOPE + ROPE) == 0
    here = whole_heads and (lax.axis_size("tx"), lax.axis_size("ty"), per_grp) == (2, 4, 2)
    layer = split_heads if here else split_positions
    layer_out = layer(
        inputs, inverse, live_len, attn_gain, latent_gain, w_query, w_down_kv, w_up_kv, w_out
    )

    at = live_len - 1 - ty * quarter
    picked = jnp.stack(
        [
            lax.dynamic_slice(
                layer_out, (i, jnp.clip(at[i], 0, quarter - 1), 0), (1, 1, half)
            ).reshape(half)
            for i in range(per_grp)
        ]
    ).astype(jnp.float32)
    inside = (at >= 0) & (at < quarter)
    picked = jnp.where(inside[:, None], picked, 0.0)
    logits = tail(
        groups, lax.axis_size("tx"), lax.axis_size("ty"), block_owner, picked, final_gain[None],
        w_vocab,
    )
    return (layer_out, logits)


def solution(mesh):
    placed = (
        P("dp", "ty", None),
        P(),
        P(),
        P(),
        P(),
        P(),
        P(),
        P("dp", ("tx", "ty")),
        P("dp", None),
        P("dp", ("tx", "ty")),
        P("dp", "tx"),
        P("dp", ("tx", "ty")),
    )
    return jax.shard_map(
        shards,
        mesh=mesh,
        in_specs=placed,
        out_specs=(P("dp", "ty", "tx"), P("dp", ("tx", "ty"))),
        check_vma=False,
    )
```

```python
import functools

import jax
import jax.numpy as jnp
from jax import lax
from jax.experimental import pallas as pl
from jax.experimental.pallas import tpu as pltpu
from jax.sharding import PartitionSpec as P

NOPE = 128
ROPE = 64
LATENT = 512
LEN = 1024
TILE = 256
EPS = 1e-06


def normalize(values, gain):
    wide = values.astype(jnp.float32)
    return wide * lax.rsqrt(jnp.mean(wide * wide, axis=-1, keepdims=True) + EPS) * gain


def dot32(left, right):
    return jnp.dot(left, right, preferred_element_type=jnp.float32)


def remote(src, dst, send, recv, **where):
    return pltpu.make_async_remote_copy(
        src_ref=src,
        dst_ref=dst,
        send_sem=send,
        recv_sem=recv,
        device_id=where,
        device_id_type=pl.DeviceIdType.MESH,
    )


def greet(**where):
    pl.semaphore_signal(
        pltpu.get_barrier_semaphore(),
        inc=1,
        device_id=where,
        device_id_type=pl.DeviceIdType.MESH,
    )


def gather_kernel(
    groups, chunks, x_ref, wq_ref, wa_ref, wb_ref, wo_ref, xs_ref, wqs_ref, was_ref, wbs_ref,
    wos_ref, z_send, z_recv, x_send, x_recv, y_send, y_recv, p_send, p_recv, a_send, a_recv,
    local,
):
    dp, tx, ty = lax.axis_index("dp"), lax.axis_index("tx"), lax.axis_index("ty")
    core = ty % 2
    partner = ty + 1 - 2 * core
    across = (ty + 2) % 4
    other = 1 - tx
    rows = x_ref.shape[1] // chunks
    steps = groups - 1

    greet(ty=partner)
    greet(ty=across)
    greet(tx=other)
    barrier = pltpu.get_barrier_semaphore()

    @pl.when(dp > 0)
    def _():
        greet(dp=dp - 1)

    @pl.when(dp < groups - 1)
    def _():
        greet(dp=dp + 1)

    ends = (dp > 0).astype(jnp.int32) + (dp < groups - 1).astype(jnp.int32)
    pl.semaphore_wait(barrier, 3 + ends)

    tensors = [
        (wq_ref, lambda g: wqs_ref.at[g]),
        (wa_ref, lambda g: was_ref.at[g, core]),
        (wb_ref, lambda g: wbs_ref.at[g]),
        (wo_ref, lambda g: wos_ref.at[g]),
    ]

    def hop(which, way, step):
        own, slot = tensors[which]
        sign = 1 - 2 * way
        block = dp - sign * step
        runs = (block >= 0) & (block < groups) & (dp + sign >= 0) & (dp + sign < groups)
        source = own if step == 0 else slot(block)
        copy = remote(
            source, slot(block), z_send.at[way, which, step], z_recv.at[way, which, step],
            dp=dp + sign,
        )
        return copy, runs

    def arrival(which, way, step):
        own, slot = tensors[which]
        sign = 1 - 2 * way
        block = dp - sign * (step + 1)
        copy = remote(
            own, slot(block), z_send.at[way, which, step], z_recv.at[way, which, step], dp=dp
        )
        return copy, (block >= 0) & (block < groups)

    def start_hop(which, step):
        for way in range(2):
            copy, runs = hop(which, way, step)
            pl.when(runs)(copy.start)

    def wait_hop(which, step):
        for way in range(2):
            copy, comes = arrival(which, way, step)
            pl.when(comes)(copy.wait_recv)

    def cut(ref, slot, prompt, k):
        return ref.at[slot, prompt, pl.ds(k * rows, rows)]

    def crossing(k, slot):
        src = x_ref.at[tx, pl.ds(k * rows, rows)]
        return remote(src, cut(xs_ref, slot, tx, k), x_send.at[k], x_recv.at[k], ty=across)

    def sideways(k, prompt):
        part = cut(xs_ref, across, prompt, k)
        return remote(part, part, y_send.at[k], y_recv.at[k], tx=other)

    def inward(k, half, slot, prompt):
        part = cut(xs_ref, slot, prompt, k)
        return remote(part, part, p_send.at[half, k], p_recv.at[half, k], ty=partner)

    def own_block(slot):
        return remote(x_ref, xs_ref.at[slot], a_send.at[0], a_recv.at[0], ty=partner)

    def down_half(side):
        part = was_ref.at[:, side]
        return remote(part, part, a_send.at[1], a_recv.at[1], ty=partner)

    for k in range(chunks):
        crossing(k, ty).start()
        if k < len(tensors):
            start_hop(k, 0)
    own_block(ty).start()
    mine = [pltpu.make_async_copy(x_ref, xs_ref.at[ty], local.at[len(tensors)])]
    for which, (own, slot) in enumerate(tensors):
        mine.append(pltpu.make_async_copy(own, slot(dp), local.at[which]))
    for copy in mine:
        copy.start()

    for k in range(chunks):
        crossing(k, across).wait_recv()
        sideways(k, tx).start()
        inward(k, 0, across, tx).start()
        if k < len(tensors):
            wait_hop(k, 0)
            if steps > 1:
                start_hop(k, 1)
    for k in range(chunks):
        sideways(k, other).wait_recv()
        inward(k, 1, across, other).start()
    for step in range(1, steps):
        for which in range(len(tensors)):
            wait_hop(which, step)
            if step + 1 < steps:
                start_hop(which, step + 1)
            if step == steps - 1 and which == 1:
                mine[2].wait()
                down_half(core).start()

    mine[0].wait()
    mine[1].wait()
    mine[3].wait()
    mine[4].wait()
    down_half(1 - core).wait_recv()
    own_block(partner).wait_recv()
    far = (partner + 2) % 4
    for k in range(chunks):
        inward(k, 0, far, tx).wait_recv()
        inward(k, 1, far, other).wait_recv()
    for step in range(steps):
        for which in range(len(tensors)):
            for way in range(2):
                copy, runs = hop(which, way, step)
                pl.when(runs)(copy.wait_send)
    for k in range(chunks):
        crossing(k, ty).wait_send()
        sideways(k, tx).wait_send()
        inward(k, 0, across, tx).wait_send()
        inward(k, 1, across, other).wait_send()
    own_block(ty).wait_send()
    down_half(core).wait_send()


def gather_all(groups, x, wq, wa, wb, wo):
    chunks = 4
    steps = max(groups - 1, 1)
    shape = lambda *dims: jax.ShapeDtypeStruct(dims, jnp.bfloat16)
    dma = pltpu.SemaphoreType.DMA
    return pl.pallas_call(
        functools.partial(gather_kernel, groups, chunks),
        in_specs=[pl.BlockSpec(memory_space=pl.ANY)] * 5,
        out_specs=[pl.BlockSpec(memory_space=pl.ANY)] * 5,
        out_shape=[
            shape(4, *x.shape),
            shape(groups, *wq.shape),
            shape(groups, 2, *wa.shape),
            shape(groups, *wb.shape),
            shape(groups, *wo.shape),
        ],
        scratch_shapes=[
            dma((2, 4, steps)), dma((2, 4, steps)),
            dma((chunks,)), dma((chunks,)), dma((chunks,)), dma((chunks,)),
            dma((2, chunks)), dma((2, chunks)), dma((2,)), dma((2,)), dma((5,)),
        ],
        compiler_params=pltpu.CompilerParams(collective_id=0, has_side_effects=True),
        cost_estimate=pl.CostEstimate(flops=0, bytes_accessed=100_000_000, transcendentals=0),
    )(x, wq, wa, wb, wo)


def load_vocab(vocab_chunk, vocab_ref, table, v_sem):
    loads = []
    for k in range(vocab_ref.shape[1] // vocab_chunk):
        cols = pl.ds(k * vocab_chunk, vocab_chunk)
        loads.append(
            pltpu.make_async_copy(vocab_ref.at[:, cols], table.at[:, cols], v_sem.at[k])
        )
        loads[-1].start()
    return loads


def next_token(
    groups, tx_size, ty_size, vocab_chunk, loads, owner_ref, picked_ref, gain_ref, out_ref, seen, full,
    rows_ref, table, part, incoming, t_send, t_recv, r_send, r_recv, l_send, l_recv,
):
    dp, tx, ty = lax.axis_index("dp"), lax.axis_index("tx"), lax.axis_index("ty")
    per_grp, half = picked_ref.shape
    block = table.shape[0]
    peers = groups * tx_size
    place = dp * tx_size + tx
    count = len(loads)

    def along_ty(k, slot):
        return remote(
            picked_ref, seen.at[slot], t_send.at[k], t_recv.at[k], ty=(ty + k) % ty_size
        )

    for k in range(1, ty_size):
        along_ty(k, ty).start()
    merged = picked_ref[...]
    for k in range(1, ty_size):
        slot = (ty + ty_size - k) % ty_size
        along_ty(k, slot).wait_recv()
        merged = merged + seen[slot]
    full[place] = merged

    def along_peers(k, slot):
        peer = (place + k) % peers
        return remote(
            full.at[place], full.at[slot], r_send.at[k], r_recv.at[k],
            dp=peer // tx_size, tx=peer % tx_size,
        )

    for k in range(1, peers):
        along_peers(k, place).start()
    for k in range(1, peers):
        along_peers(k, (place + peers - k) % peers).wait_recv()
    for g in range(groups):
        for t in range(tx_size):
            rows_ref[g * per_grp : (g + 1) * per_grp, t * half : (t + 1) * half] = full[
                g * tx_size + t
            ]
    final = normalize(rows_ref[...], gain_ref[...])
    owner = owner_ref[dp]
    mine = jnp.zeros((groups * per_grp, block), jnp.float32)
    for g in range(groups):
        mine = jnp.where(owner == g, final[:, g * block : (g + 1) * block], mine)
    mine = mine.astype(jnp.bfloat16)
    for k in range(count):
        loads[k].wait()
        cols = slice(k * vocab_chunk, (k + 1) * vocab_chunk)
        logits = dot32(mine, table[:, cols].astype(jnp.bfloat16))
        for g in range(groups):
            part[g, :, cols] = logits[g * per_grp : (g + 1) * per_grp]

    def along_dp(k, slot):
        peer = (dp + k) % groups
        return remote(part.at[peer], incoming.at[slot], l_send.at[k], l_recv.at[k], dp=peer)

    for k in range(1, groups):
        along_dp(k, dp).start()
    total = part[dp]
    for k in range(1, groups):
        slot = (dp + groups - k) % groups
        along_dp(k, slot).wait_recv()
        total = total + incoming[slot]
    out_ref[...] = total
    for k in range(1, ty_size):
        along_ty(k, ty).wait_send()
    for k in range(1, peers):
        along_peers(k, place).wait_send()
    for k in range(1, groups):
        along_dp(k, dp).wait_send()


def tail_kernel(
    groups, tx_size, ty_size, vocab_chunk, owner_ref, picked_ref, gain_ref, vocab_ref, out_ref,
    seen, full, rows_ref, table, part, incoming, t_send, t_recv, r_send, r_recv, l_send, l_recv,
    v_sem,
):
    dp, tx, ty = lax.axis_index("dp"), lax.axis_index("tx"), lax.axis_index("ty")
    peers = groups * tx_size
    place = dp * tx_size + tx
    loads = load_vocab(vocab_chunk, vocab_ref, table, v_sem)
    for k in range(1, ty_size):
        greet(ty=(ty + k) % ty_size)
    for k in range(1, peers):
        peer = (place + k) % peers
        greet(dp=peer // tx_size, tx=peer % tx_size)
    pl.semaphore_wait(pltpu.get_barrier_semaphore(), ty_size + peers - 2)
    next_token(
        groups, tx_size, ty_size, vocab_chunk, loads, owner_ref, picked_ref, gain_ref, out_ref,
        seen, full, rows_ref, table, part, incoming, t_send, t_recv, r_send, r_recv, l_send,
        l_recv,
    )


def close_kernel(
    groups, tx_size, ty_size, vocab_chunk, owner_ref, live_ref, o_ref, wo_ref, residual_ref,
    gain_ref, vocab_ref, hidden_ref, out_ref,
    heard, wos, total, picked_ref, o_send, o_recv, w_sem, seen, full, rows_ref, table, part,
    incoming, t_send, t_recv, r_send, r_recv, l_send, l_recv, v_sem,
):
    dp, tx, ty = lax.axis_index("dp"), lax.axis_index("tx"), lax.axis_index("ty")
    plane = tx_size * ty_size
    spot = tx * ty_size + ty
    per_grp, quarter, half = residual_ref.shape
    heads_width = wos.shape[-1]

    weights = pltpu.make_async_copy(wo_ref, wos, w_sem.at[0])
    weights.start()
    for k in range(1, plane):
        peer = (spot + k) % plane
        greet(tx=peer // ty_size, ty=peer % ty_size)
    for k in range(1, groups):
        for t in range(tx_size):
            greet(dp=(dp + k) % groups, tx=t)
    pl.semaphore_wait(pltpu.get_barrier_semaphore(), plane - 1 + (groups - 1) * tx_size)

    def heads_of(k, slot):
        peer = (spot + k) % plane
        return remote(
            o_ref.at[peer % ty_size], heard.at[slot], o_send.at[k], o_recv.at[k],
            tx=peer // ty_size, ty=peer % ty_size,
        )

    for k in range(1, plane):
        heads_of(k, spot).start()
    loads = load_vocab(vocab_chunk, vocab_ref, table, v_sem)
    weights.wait()
    for k in (0,) + tuple(range(1, plane)):
        source = (spot + plane - k) % plane
        if k:
            heads_of(k, source).wait_recv()
        for p in range(per_grp):
            block = o_ref[ty, p] if k == 0 else heard[source, p]
            term = lax.dot_general(
                block, wos[source], (((1,), (1,)), ((), ())),
                preferred_element_type=jnp.float32,
            )
            total[p] = term if k == 0 else total[p] + term
    row = lax.broadcasted_iota(jnp.int32, (quarter, half), 0)
    for p in range(per_grp):
        hidden = (residual_ref[p].astype(jnp.float32) + total[p]).astype(jnp.bfloat16)
        hidden_ref[p] = hidden
        last = row == live_ref[p] - 1 - ty * quarter
        picked_ref[p : p + 1, :] = jnp.sum(
            jnp.where(last, hidden.astype(jnp.float32), 0.0), axis=0, keepdims=True
        )
    next_token(
        groups, tx_size, ty_size, vocab_chunk, loads, owner_ref, picked_ref, gain_ref, out_ref,
        seen, full, rows_ref, table, part, incoming, t_send, t_recv, r_send, r_recv, l_send,
        l_recv,
    )
    for k in range(1, plane):
        heads_of(k, spot).wait_send()


def close(groups, tx_size, ty_size, owner, live, mixed, wo, residual, gain, vocab):
    per_grp, quarter, half = residual.shape
    block, words = vocab.shape
    vocab_chunk = 512
    peers = groups * tx_size
    plane = tx_size * ty_size
    dma = pltpu.SemaphoreType.DMA
    vmem = pl.BlockSpec(memory_space=pltpu.VMEM)
    smem = pl.BlockSpec(memory_space=pltpu.SMEM)
    hbm = pl.BlockSpec(memory_space=pl.ANY)
    return pl.pallas_call(
        functools.partial(close_kernel, groups, tx_size, ty_size, vocab_chunk),
        in_specs=[smem, smem, vmem, hbm, vmem, vmem, hbm],
        out_specs=[vmem, vmem],
        out_shape=[
            jax.ShapeDtypeStruct(residual.shape, jnp.bfloat16),
            jax.ShapeDtypeStruct((per_grp, words), jnp.float32),
        ],
        scratch_shapes=[
            pltpu.VMEM((plane,) + mixed.shape[1:], jnp.bfloat16),
            pltpu.VMEM(wo.shape, jnp.bfloat16),
            pltpu.VMEM(residual.shape, jnp.float32),
            pltpu.VMEM((per_grp, half), jnp.float32),
            dma((plane,)), dma((plane,)), dma((1,)),
            pltpu.VMEM((ty_size, per_grp, half), jnp.float32),
            pltpu.VMEM((peers, per_grp, half), jnp.float32),
            pltpu.VMEM((groups * per_grp, half * tx_size), jnp.float32),
            pltpu.VMEM((block, words), jnp.float32),
            pltpu.VMEM((groups, per_grp, words), jnp.float32),
            pltpu.VMEM((groups, per_grp, words), jnp.float32),
            dma((ty_size,)), dma((ty_size,)), dma((peers,)), dma((peers,)),
            dma((groups,)), dma((groups,)), dma((words // vocab_chunk,)),
        ],
        compiler_params=pltpu.CompilerParams(
            collective_id=3, has_side_effects=True, vmem_limit_bytes=48 * 1024 * 1024
        ),
        cost_estimate=pl.CostEstimate(
            flops=3_000_000_000, bytes_accessed=24_000_000, transcendentals=0
        ),
    )(owner, live, mixed, wo, residual, gain, vocab)


def tail(groups, tx_size, ty_size, owner, picked, gain, vocab):
    per_grp, half = picked.shape
    block, words = vocab.shape
    vocab_chunk = 512
    peers = groups * tx_size
    dma = pltpu.SemaphoreType.DMA
    vmem = pl.BlockSpec(memory_space=pltpu.VMEM)
    return pl.pallas_call(
        functools.partial(tail_kernel, groups, tx_size, ty_size, vocab_chunk),
        in_specs=[
            pl.BlockSpec(memory_space=pltpu.SMEM), vmem, vmem, pl.BlockSpec(memory_space=pl.ANY),
        ],
        out_specs=vmem,
        out_shape=jax.ShapeDtypeStruct((per_grp, words), jnp.float32),
        scratch_shapes=[
            pltpu.VMEM((ty_size, per_grp, half), jnp.float32),
            pltpu.VMEM((peers, per_grp, half), jnp.float32),
            pltpu.VMEM((groups * per_grp, half * tx_size), jnp.float32),
            pltpu.VMEM((block, words), jnp.float32),
            pltpu.VMEM((groups, per_grp, words), jnp.float32),
            pltpu.VMEM((groups, per_grp, words), jnp.float32),
            dma((ty_size,)), dma((ty_size,)), dma((peers,)), dma((peers,)),
            dma((groups,)), dma((groups,)), dma((words // vocab_chunk,)),
        ],
        compiler_params=pltpu.CompilerParams(
            collective_id=1, has_side_effects=True, vmem_limit_bytes=40 * 1024 * 1024
        ),
        cost_estimate=pl.CostEstimate(
            flops=100_000_000, bytes_accessed=16_000_000, transcendentals=0
        ),
    )(owner, picked, gain, vocab)


def layer_kernel(
    heads, live_ref, x_ref, again_ref, lgain_ref, cos_ref, sin_ref,
    wq_ref, wa_ref, wb_ref, keep_ref, give_ref, o_ref, wos_ref, h_ref, k_ref, v_ref,
    send, recv, local,
):
    prompt, tile = pl.program_id(0), pl.program_id(1)
    moment = prompt * (LEN // TILE) + tile
    tx, ty = lax.axis_index("tx"), lax.axis_index("ty")
    partner = ty + 1 - 2 * (ty % 2)
    across = (ty + 2) % 4
    far = (partner + 2) % 4
    other = 1 - tx

    def move(n, source, slot_tx, slot_ty, **where):
        return remote(source, wos_ref.at[slot_tx, slot_ty], send.at[n], recv.at[n], **where)

    def passed(n, slot_tx, slot_ty, **where):
        return move(n, wos_ref.at[slot_tx, slot_ty], slot_tx, slot_ty, **where)

    @pl.when(moment == 0)
    def _():
        greet(tx=other)
        greet(ty=partner)
        greet(ty=across)
        pl.semaphore_wait(pltpu.get_barrier_semaphore(), 3)
        move(0, give_ref, tx, ty, tx=other).start()
        move(1, keep_ref, tx, ty, ty=across).start()
        move(2, keep_ref, tx, ty, ty=partner).start()
        pltpu.make_async_copy(keep_ref, wos_ref.at[tx, ty], local.at[0]).start()

    @pl.when(moment == 3)
    def _():
        move(0, give_ref, other, ty, tx=other).wait_recv()
        passed(3, other, ty, ty=across).start()
        passed(4, other, ty, ty=partner).start()
        move(1, keep_ref, tx, across, ty=across).wait_recv()
        passed(5, tx, across, ty=partner).start()

    @pl.when(moment == 6)
    def _():
        move(3, keep_ref, other, across, ty=across).wait_recv()
        passed(6, other, across, ty=partner).start()

    width = x_ref.shape[-1]
    h_ref[...] = normalize(x_ref[0, 0], again_ref[...]).astype(jnp.bfloat16)

    cosine, sine = cos_ref[...], sin_ref[...]
    lane = lax.broadcasted_iota(jnp.int32, (TILE, 128), 1)

    def rotate(block):
        swapped = jnp.where(
            lane % ROPE < ROPE // 2,
            pltpu.roll(block, 128 - ROPE // 2, 1),
            pltpu.roll(block, ROPE // 2, 1),
        )
        return block * cosine + swapped * sine

    down = dot32(h_ref[...], wa_ref[...])
    latent = normalize(down[:, :LATENT], lgain_ref[...]).astype(jnp.bfloat16)
    key_rope = rotate(down[:, LATENT:]).astype(jnp.bfloat16)
    key_val = dot32(latent, wb_ref[...]).astype(jnp.bfloat16)
    here = pl.ds(pl.multiple_of(tile * TILE, TILE), TILE)
    for head in range(heads):
        k_ref[head, here, :NOPE] = key_val[:, 2 * head * NOPE : (2 * head + 1) * NOPE]
        k_ref[head, here, NOPE:] = key_rope
        v_ref[head, here, :] = key_val[:, (2 * head + 1) * NOPE : (2 * head + 2) * NOPE]

    queries = dot32(h_ref[...], wq_ref[...])
    nope = queries[:, : heads * NOPE].astype(jnp.bfloat16)
    query = []
    for head in range(heads):
        base = heads * NOPE + (head // 2) * 128
        turned = rotate(queries[:, base : base + 128])
        mine = jnp.where(lane // ROPE == head % 2, turned, 0.0).astype(jnp.bfloat16)
        query.append(jnp.concatenate([nope[:, head * NOPE : (head + 1) * NOPE], mine], axis=1))

    live = live_ref[prompt]
    scale = (NOPE + ROPE) ** (-0.5)
    for count in range(1, LEN // TILE + 1):

        @pl.when(tile == count - 1)
        def _():
            span = count * TILE
            i = lax.broadcasted_iota(jnp.int32, (TILE, span), 0) + (count - 1) * TILE
            j = lax.broadcasted_iota(jnp.int32, (TILE, span), 1)
            allowed = (j <= i) & (j < live)
            for head in range(heads):
                score = lax.dot_general(
                    query[head], k_ref[head, :span, :], (((1,), (1,)), ((), ())),
                    preferred_element_type=jnp.float32,
                )
                score = jnp.where(allowed, score * scale, -1e30)
                expo = jnp.exp(score - jnp.max(score, axis=-1, keepdims=True))
                prob = expo * (1.0 / jnp.sum(expo, axis=-1, keepdims=True))
                out = dot32(prob.astype(jnp.bfloat16), v_ref[head, :span, :])
                o_ref[0, 0, :, head * NOPE : (head + 1) * NOPE] = out.astype(jnp.bfloat16)

    @pl.when(moment == 7)
    def _():
        move(2, keep_ref, tx, partner, ty=partner).wait_recv()
        move(4, keep_ref, other, partner, ty=partner).wait_recv()
        move(5, keep_ref, tx, far, ty=partner).wait_recv()
        move(6, keep_ref, other, far, ty=partner).wait_recv()
        move(0, give_ref, tx, ty, tx=other).wait_send()
        move(1, keep_ref, tx, ty, ty=across).wait_send()
        move(2, keep_ref, tx, ty, ty=partner).wait_send()
        passed(3, other, ty, ty=across).wait_send()
        passed(4, other, ty, ty=partner).wait_send()
        passed(5, tx, across, ty=partner).wait_send()
        passed(6, other, across, ty=partner).wait_send()
        pltpu.make_async_copy(keep_ref, wos_ref.at[tx, ty], local.at[0]).wait()


def attend(
    live, x, again, lgain, cosine, sine, wq, wa, wb, keep, give
):
    _, per_grp, _, width = x.shape
    heads = wb.shape[1] // (2 * NOPE)
    whole = lambda a: pl.BlockSpec(a.shape, lambda p, t: (0,) * a.ndim)
    smem = pl.BlockSpec(memory_space=pltpu.SMEM)
    return pl.pallas_call(
        functools.partial(layer_kernel, heads),
        grid=(per_grp, LEN // TILE),
        in_specs=[
            smem,
            pl.BlockSpec((1, 1, TILE, width), lambda p, t: (t, p, 0, 0)),
            whole(again),
            whole(lgain),
            pl.BlockSpec((TILE, 128), lambda p, t: (t, 0)),
            pl.BlockSpec((TILE, 128), lambda p, t: (t, 0)),
            whole(wq),
            whole(wa),
            whole(wb),
            pl.BlockSpec(memory_space=pl.ANY),
            pl.BlockSpec(memory_space=pl.ANY),
        ],
        out_specs=[
            pl.BlockSpec((1, 1, TILE, heads * NOPE), lambda p, t: (t, p, 0, 0)),
            pl.BlockSpec(memory_space=pl.ANY),
        ],
        out_shape=[
            jax.ShapeDtypeStruct((LEN // TILE, per_grp, TILE, heads * NOPE), jnp.bfloat16),
            jax.ShapeDtypeStruct((2, 4) + keep.shape, jnp.bfloat16),
        ],
        scratch_shapes=[
            pltpu.VMEM((TILE, width), jnp.bfloat16),
            pltpu.VMEM((heads, LEN, 2 * NOPE), jnp.bfloat16),
            pltpu.VMEM((heads, LEN, NOPE), jnp.bfloat16),
            pltpu.SemaphoreType.DMA((7,)),
            pltpu.SemaphoreType.DMA((7,)),
            pltpu.SemaphoreType.DMA((1,)),
        ],
        compiler_params=pltpu.CompilerParams(
            collective_id=2, has_side_effects=True, vmem_limit_bytes=48 * 1024 * 1024
        ),
        cost_estimate=pl.CostEstimate(
            flops=20_000_000_000, bytes_accessed=16_000_000, transcendentals=4_000_000
        ),
    )(live, x, again, lgain, cosine, sine, wq, wa, wb, keep, give)


def rotate_half(values, position):
    half_dim = values.shape[-1] // 2
    frequency = 10000.0 ** (-jnp.arange(half_dim, dtype=jnp.float32) / half_dim)
    angles = position.astype(jnp.float32)[..., None] * frequency
    cosine = jnp.cos(angles)
    sine = jnp.sin(angles)
    first_half = values[..., :half_dim]
    second_half = values[..., half_dim:]
    return jnp.concatenate(
        [first_half * cosine - second_half * sine, first_half * sine + second_half * cosine],
        axis=-1,
    )


def split_positions(
    inputs, inverse, live_len, attn_gain, latent_gain, w_query, w_down_kv, w_up_kv, w_out
):
    groups = lax.axis_size("dp")

    def arrange(gathered):
        block_rows = gathered.shape[0] // groups
        blocks = gathered.reshape((groups, block_rows) + gathered.shape[1:])
        return jnp.take(blocks, inverse, axis=0).reshape(gathered.shape)

    query_w, down_w, up_w, out_w = (
        lax.all_gather(w_query.astype(jnp.bfloat16), "dp", axis=0, tiled=True),
        lax.all_gather(w_down_kv.astype(jnp.bfloat16), "dp", axis=0, tiled=True),
        lax.all_gather(w_up_kv.astype(jnp.bfloat16), "dp", axis=0, tiled=True),
        lax.all_gather(w_out.astype(jnp.bfloat16), "dp", axis=0, tiled=True),
    )
    query_w = arrange(query_w)
    down_w = arrange(down_w)
    up_w = arrange(up_w)
    out_w = arrange(out_w)
    query_w, up_w = (
        lax.all_gather(query_w, "ty", axis=1, tiled=True),
        lax.all_gather(up_w, "ty", axis=1, tiled=True),
    )
    per_grp, quarter, width = inputs.shape
    heads = query_w.shape[1] // (NOPE + ROPE)
    position = lax.axis_index("ty") * quarter + jnp.arange(quarter, dtype=jnp.int32)
    flat_rows = inputs.reshape(per_grp * quarter, width)
    normed = normalize(flat_rows, attn_gain).astype(jnp.bfloat16)
    queries = jnp.dot(normed, query_w, preferred_element_type=jnp.float32).reshape(
        per_grp, quarter, heads, NOPE + ROPE
    )
    queries = jnp.concatenate(
        [queries[..., :NOPE], rotate_half(queries[..., NOPE:], position[None, :, None])], axis=-1
    ).astype(jnp.bfloat16)
    down_proj = jnp.dot(normed, down_w, preferred_element_type=jnp.float32).reshape(
        per_grp, quarter, LATENT + ROPE
    )
    latent = normalize(down_proj[..., :LATENT], latent_gain).astype(jnp.bfloat16)
    key_rope = rotate_half(down_proj[..., LATENT:], position[None, :]).astype(jnp.bfloat16)
    gathered = lax.all_gather(
        jnp.concatenate([latent, key_rope], axis=-1), "ty", axis=1, tiled=True
    )
    key_val = jnp.dot(gathered[..., :LATENT], up_w, preferred_element_type=jnp.float32).astype(
        jnp.bfloat16
    )
    rope_all = gathered[..., LATENT:]
    key_val = key_val.reshape(per_grp, LEN, heads, 2, NOPE)
    key_nope = key_val[:, :, :, 0]
    values = key_val[:, :, :, 1]
    score_scale = (NOPE + ROPE) ** (-0.5)
    scores = (
        jnp.einsum(
            "pqhd,pkhd->phqk", queries[..., :NOPE], key_nope, preferred_element_type=jnp.float32
        )
        + jnp.einsum(
            "pqhd,pkd->phqk", queries[..., NOPE:], rope_all, preferred_element_type=jnp.float32
        )
    ) * score_scale
    key_pos = jnp.arange(LEN, dtype=jnp.int32)
    allowed = (key_pos[None, None, :] <= position[None, :, None]) & (
        key_pos[None, None, :] < live_len[:, None, None]
    )
    scores = jnp.where(allowed[:, None], scores, -1e30)
    top = jnp.max(scores, axis=-1, keepdims=True)
    expo = jnp.exp(scores - top)
    softmax_w = (expo / jnp.sum(expo, axis=-1, keepdims=True)).astype(jnp.bfloat16)
    attended = jnp.einsum(
        "phqk,pkhd->pqhd", softmax_w, values, preferred_element_type=jnp.float32
    ).astype(jnp.bfloat16)
    attended = attended.reshape(per_grp * quarter, heads * NOPE)
    own_width = width // lax.axis_size("tx")
    col_start = lax.axis_index("tx") * own_width
    partial_value = lax.dot_general(
        attended, out_w, (((1,), (1,)), ((), ())), preferred_element_type=jnp.float32
    ).reshape(per_grp, quarter, width)
    summed = lax.psum_scatter(partial_value, "tx", scatter_dimension=2, tiled=True)
    residual = lax.dynamic_slice_in_dim(inputs, col_start, own_width, 2)
    layer_out = (residual.astype(jnp.float32) + summed).astype(jnp.bfloat16)
    return layer_out


def split_heads(
    inputs, inverse, live_len, attn_gain, latent_gain, w_query, w_down_kv, w_up_kv, w_out,
    block_owner, final_gain, w_vocab,
):
    groups = lax.axis_size("dp")
    tx_size, ty_size = lax.axis_size("tx"), lax.axis_size("ty")
    tx, ty = lax.axis_index("tx"), lax.axis_index("ty")
    per_grp, quarter, width = inputs.shape
    half = width // tx_size
    rows = w_query.shape[0]
    heads = w_query.shape[1] // (NOPE + ROPE)
    wq = w_query.astype(jnp.bfloat16).reshape(rows, heads, NOPE + ROPE)
    rope_q = wq[:, :, NOPE:].reshape(rows, heads * ROPE)
    rope_q = jnp.pad(rope_q, ((0, 0), (0, -(heads * ROPE) % 128)))
    wq = jnp.concatenate([wq[:, :, :NOPE].reshape(rows, heads * NOPE), rope_q], axis=1)
    wa = lax.dynamic_slice_in_dim(w_down_kv, (ty % 2) * (rows // 2), rows // 2, 0)
    wa = jnp.concatenate([wa, wa[:, LATENT:]], axis=1).astype(jnp.bfloat16)
    piece = w_out.shape[1] // ty_size
    wo = lax.dynamic_slice_in_dim(w_out, ty * piece, piece, 1).astype(jnp.bfloat16)
    x_all, wq, wa, wb, wo = gather_all(
        groups, inputs, wq, wa, w_up_kv.astype(jnp.bfloat16), wo
    )
    wq, wa, wb = (
        jnp.take(w, inverse, axis=0).reshape(-1, w.shape[-1]) for w in (wq, wa, wb)
    )

    position = jnp.arange(LEN, dtype=jnp.float32)
    frequency = 10000.0 ** (-jnp.arange(ROPE // 2, dtype=jnp.float32) / (ROPE // 2))
    angles = position[:, None] * frequency
    cosine, sine = jnp.cos(angles), jnp.sin(angles)
    cosine = jnp.concatenate([cosine] * 4, axis=1)
    sine = jnp.concatenate([-sine, sine, -sine, sine], axis=1)

    share = groups // tx_size

    def model_rows(which):
        blocks = lax.dynamic_slice_in_dim(inverse, which * share, share)
        return jnp.take(wo, blocks, axis=0).reshape(half, piece)

    mixed, wo = attend(
        live_len, x_all, attn_gain[None], latent_gain[None], cosine, sine,
        wq, wa, wb, model_rows(tx), model_rows(1 - tx),
    )
    residual = lax.dynamic_slice_in_dim(inputs, tx * half, half, 2)
    return tuple(
        close(
            groups, tx_size, ty_size, block_owner, live_len, mixed,
            wo.reshape((tx_size * ty_size,) + wo.shape[2:]), residual, final_gain[None], w_vocab,
        )
    )


def shards(
    inputs,
    lengths,
    prompt_deal,
    block_owner,
    attn_gain,
    latent_gain,
    final_gain,
    w_query,
    w_down_kv,
    w_up_kv,
    w_out,
    w_vocab,
):
    groups = lax.axis_size("dp")
    dp, tx, ty = lax.axis_index("dp"), lax.axis_index("tx"), lax.axis_index("ty")
    per_grp, quarter, width = inputs.shape
    half = width // lax.axis_size("tx")
    order = jnp.arange(groups, dtype=jnp.int32)
    inverse = jnp.sum(
        jnp.where(block_owner[None, :] == order[:, None], order[None, :], 0), axis=1
    ).astype(jnp.int32)
    slots = dp * per_grp + jnp.arange(per_grp, dtype=jnp.int32)
    live_len = jnp.take(lengths, jnp.take(prompt_deal, slots))

    whole_heads = w_query.shape[1] % (NOPE + ROPE) == 0
    here = whole_heads and (lax.axis_size("tx"), lax.axis_size("ty"), per_grp) == (2, 4, 2)
    arrays = (
        inputs, inverse, live_len, attn_gain, latent_gain, w_query, w_down_kv, w_up_kv, w_out
    )
    if here and groups > 2 and groups % 2 == 0:
        return split_heads(*arrays, block_owner, final_gain, w_vocab)
    layer_out = split_positions(*arrays)

    at = live_len - 1 - ty * quarter
    picked = jnp.stack(
        [
            lax.dynamic_slice(
                layer_out, (i, jnp.clip(at[i], 0, quarter - 1), 0), (1, 1, half)
            ).reshape(half)
            for i in range(per_grp)
        ]
    ).astype(jnp.float32)
    inside = (at >= 0) & (at < quarter)
    picked = jnp.where(inside[:, None], picked, 0.0)
    logits = tail(
        groups, lax.axis_size("tx"), lax.axis_size("ty"), block_owner, picked, final_gain[None],
        w_vocab,
    )
    return (layer_out, logits)


def solution(mesh):
    placed = (
        P("dp", "ty", None),
        P(),
        P(),
        P(),
        P(),
        P(),
        P(),
        P("dp", ("tx", "ty")),
        P("dp", None),
        P("dp", ("tx", "ty")),
        P("dp", "tx"),
        P("dp", ("tx", "ty")),
    )
    return jax.shard_map(
        shards,
        mesh=mesh,
        in_specs=placed,
        out_specs=(P("dp", "ty", "tx"), P("dp", ("tx", "ty"))),
        check_vma=False,
    )
```
